32 devices in a mesh: island: 4 (over x, core), fsdp: 8 (over z, y).
Axes of the slice: x: 2, y: 2, z: 4, core: 2. Of those that a mesh axis runs over, the one named last changes fastest.
Arguments:
- local_weights: bfloat16 [4, 64, 8192], P('island', 'fsdp'), may hold values from -6 to 6
- base_master: float32 [64, 8192], P('fsdp'), may hold values from -6 to 6
- momentum: float32 [64, 8192], P('fsdp'), may hold values from -4 to 4
Outputs:
- new_master: float32 [64, 8192], P('fsdp')
- new_momentum: float32 [64, 8192], P('fsdp')
- new_base: bfloat16 [64, 8192], replicated
The draws below stay inside these ranges and needn't reach their ends.
All inputs are finite; a program needn't handle non-finite values.
Results may differ from the reference program's by a relative error of at most 0.02.
Values may be sent and summed in bfloat16 or wider, within the bound.
A program may use at most 64 MiB of HBM per device.

```python
import jax
import jax.numpy as jnp

D = 8192
BLOCK = 128
ROWS = 64
ISLANDS = 4


def shard_levels(own_key, dims, shards, smallest, high):
    level = 1.0
    for axis_at, shards_of in shards:
        steps = jax.random.uniform(jax.random.fold_in(jax.random.fold_in(own_key, 6), axis_at), (shards_of,), jnp.float32, smallest / len(shards), high / len(shards))
        level = level * jnp.repeat(jnp.exp(steps), dims[axis_at] // shards_of).reshape((-1,) + (1,) * (len(dims) - 1 - axis_at))
    return level


def gaussian(stream_key, dims, width, limit, split=(), kind=jnp.bfloat16):
    entries = width * jax.random.normal(stream_key, dims, jnp.float32)
    if split:
        entries = entries * shard_levels(stream_key, dims, split, -0.22, 0.18)
    return jnp.clip(entries, -limit, limit).astype(kind)


def setup_inputs(seed: int = 0) -> dict:
    seeds = jax.random.split(jax.random.key(seed), 4)
    local_weights = gaussian(seeds[0], (ISLANDS, ROWS, D), 1.0, 6.0, ((0, 4), (1, 8)))
    base_master = gaussian(seeds[1], (ROWS, D), 1.0, 6.0, ((0, 8),), jnp.float32)
    momentum = gaussian(seeds[2], (ROWS, D), 0.5, 4.0, ((0, 8),), jnp.float32)
    return dict(local_weights=local_weights, base_master=base_master, momentum=momentum)


epsilon = 1e-6
code_limit = 31.0
momentum_decay = 0.9
outer_rate = 0.7


def decode_group(outer_grad):
    blocks = outer_grad.reshape(outer_grad.shape[0], D // BLOCK, BLOCK)
    largest = jnp.max(jnp.abs(blocks), axis=2, keepdims=True)
    block_scale = (largest + epsilon) / code_limit
    code_values = (blocks / block_scale).astype(jnp.bfloat16)
    return (code_values.astype(jnp.float32) * block_scale).reshape(outer_grad.shape)


def reference(local_weights, base_master, momentum):
    summed = jnp.zeros(base_master.shape, jnp.float32)
    for group_index in range(ISLANDS):
        outer_grad = base_master - local_weights[group_index].astype(jnp.float32)
        summed = summed + decode_group(outer_grad)
    averaged = summed / ISLANDS
    new_momentum = momentum_decay * momentum + averaged
    new_master = base_master - outer_rate * (averaged + momentum_decay * new_momentum)
    return new_master, new_momentum, new_master.astype(jnp.bfloat16)
```

```python
import functools

import jax
import jax.numpy as jnp
from jax import lax
from jax.experimental import pallas as pl
from jax.experimental.pallas import tpu as pltpu
from jax.sharding import PartitionSpec as P

BLOCK = 128
CHUNKS = 2
UNROLL = 8

epsilon = 1e-06
code_limit = 31.0
momentum_decay = 0.9
outer_rate = 0.7


def flip(index, mask):
    out = index
    bit = 1
    while bit <= mask:
        if mask & bit:
            out = out + bit - 2 * bit * lax.rem(lax.div(index, bit), 2)
        bit *= 2
    return out


def decoded(outer_grad):
    largest = jnp.max(jnp.abs(outer_grad), axis=1, keepdims=True)
    block_scale = (largest + epsilon) / code_limit
    coded = (outer_grad / block_scale).astype(jnp.bfloat16)
    return coded.astype(jnp.float32) * block_scale


def kernel(
    groups,
    n,
    weights_in,
    base_in,
    moment_in,
    master_out,
    moment_out,
    rows_out,
    weights,
    base,
    moment,
    load_sem,
    island_send,
    island_recv,
    line_send,
    pair_send,
    core_send,
    rows_recv,
):
    isl = lax.axis_index("island")
    shard = lax.axis_index("fsdp")
    mine = lax.rem(isl, 2)
    width = base.shape[1]
    half = width // 2
    piece = half // CHUNKS
    lines = range(2, n, 2)

    loads = [
        pltpu.make_async_copy(weights_in.at[0], weights.at[isl], load_sem.at[0]),
        pltpu.make_async_copy(base_in, base, load_sem.at[1]),
        pltpu.make_async_copy(moment_in, moment, load_sem.at[2]),
    ]
    for load in loads:
        load.start()

    barrier = pltpu.get_barrier_semaphore()
    partners = [(flip(isl, m), shard) for m in range(1, groups)]
    partners += [(isl, flip(shard, m)) for m in (1, *lines)]
    for partner in partners:
        pl.semaphore_signal(barrier, inc=1, device_id=partner, device_id_type=pl.DeviceIdType.MESH)
    loads[0].wait()
    pl.semaphore_wait(barrier, len(partners))

    def columns(side, k):
        return pl.ds(pl.multiple_of(side * half + k * piece, BLOCK), piece)

    def remote(ref, send, recv, partner):
        return pltpu.make_async_remote_copy(
            src_ref=ref,
            dst_ref=ref,
            send_sem=send,
            recv_sem=recv,
            device_id=partner,
            device_id_type=pl.DeviceIdType.MESH,
        )

    sent = []

    def send(copy):
        copy.start()
        sent.append(copy)

    def island_copy(source, side, k, mask, send_at, recv_at):
        return remote(
            weights.at[source, :, columns(side, k)],
            island_send.at[send_at],
            island_recv.at[recv_at],
            (flip(isl, mask), shard),
        )

    def rows_copy(mask, side, k, send_sem, recv_at, partner):
        return remote(
            rows_out.at[flip(shard, mask), :, columns(side, k)],
            send_sem,
            rows_recv.at[recv_at],
            partner,
        )

    for k in range(CHUNKS):
        for m in range(2, groups):
            side = mine if m % 2 == 0 else 1 - mine
            send(island_copy(isl, side, k, m, (m, 0, k), (m, 0, k)))
        send(island_copy(isl, 1 - mine, k, 1, (1, 0, k), (1, 0, k)))
    for k in range(CHUNKS):
        send(island_copy(isl, mine, k, 1, (1, 1, k), (1, 1, k)))
    loads[1].wait()
    loads[2].wait()

    def update(side, k):
        start = side * half + k * piece

        def step(t, carry):
            for u in range(UNROLL):
                at = pl.ds(pl.multiple_of(start + (t * UNROLL + u) * BLOCK, BLOCK), BLOCK)
                held = base[:, at]
                summed = None
                for m in range(groups):
                    term = decoded(held - weights[flip(isl, m), :, at].astype(jnp.float32))
                    summed = term if summed is None else summed + term
                averaged = summed / groups
                fresh_moment = momentum_decay * moment[:, at] + averaged
                fresh_master = held - outer_rate * (averaged + momentum_decay * fresh_moment)
                moment_out[:, at] = fresh_moment
                master_out[:, at] = fresh_master
                rows_out[shard, :, at] = fresh_master.astype(jnp.bfloat16)
            return carry

        lax.fori_loop(0, piece // (BLOCK * UNROLL), step, 0)

    def wait_island(mask, rel, k):
        island_copy(
            flip(isl, mask), mine if rel == 0 else 1 - mine, k, 1, (mask, rel, k), (mask, rel, k)
        ).wait_recv()

    def wait_rows(mask, rel, k):
        rows_copy(
            mask, mine if rel == 0 else 1 - mine, k, core_send.at[mask, k], (mask, rel, k), (flip(isl, 1), shard)
        ).wait_recv()

    pair = (isl, flip(shard, 1))
    core = (flip(isl, 1), shard)

    for k in range(CHUNKS):
        for m in range(1, groups):
            wait_island(m, 0, k)
            if m > 1:
                send(island_copy(flip(isl, m), mine, k, 1, (m, 1, k), (m ^ 1, 1, k)))
        update(mine, k)
        for m in lines:
            send(rows_copy(0, mine, k, line_send.at[m // 2, k], (m, 0, k), (isl, flip(shard, m))))
        send(rows_copy(0, mine, k, pair_send.at[0, k], (1, 0, k), pair))

    for k in range(CHUNKS):
        for m in range(1, groups):
            wait_island(m, 1, k)
        update(1 - mine, k)

    for k in range(CHUNKS):
        wait_rows(1, 0, k)
        send(rows_copy(1, mine, k, core_send.at[1, k], (1, 1, k), core))
        for m in lines:
            wait_rows(m, 0, k)
            send(rows_copy(m, mine, k, pair_send.at[m // 2, k], (m + 1, 0, k), pair))
            send(rows_copy(m, mine, k, core_send.at[m, k], (m, 1, k), core))
    for k in range(CHUNKS):
        for m in lines:
            wait_rows(m + 1, 0, k)
            send(rows_copy(m + 1, mine, k, core_send.at[m + 1, k], (m + 1, 1, k), core))
    for k in range(CHUNKS):
        for m in range(1, n):
            wait_rows(m, 1, k)
    for copy in sent:
        copy.wait_send()


def solution(mesh):
    groups, n = mesh.shape["island"], mesh.shape["fsdp"]

    def on_device(local_weights, base_master, momentum):
        rows, width = base_master.shape
        vmem = pl.BlockSpec(memory_space=pltpu.VMEM)
        hbm = pl.BlockSpec(memory_space=pltpu.HBM)
        new_master, new_momentum, all_rows = pl.pallas_call(
            functools.partial(kernel, groups, n),
            out_shape=(
                jax.ShapeDtypeStruct((rows, width), jnp.float32),
                jax.ShapeDtypeStruct((rows, width), jnp.float32),
                jax.ShapeDtypeStruct((n, rows, width), jnp.bfloat16),
            ),
            in_specs=[hbm] * 3,
            out_specs=(vmem,) * 3,
            scratch_shapes=[
                pltpu.VMEM((groups, rows, width), jnp.bfloat16),
                pltpu.VMEM((rows, width), jnp.float32),
                pltpu.VMEM((rows, width), jnp.float32),
                pltpu.SemaphoreType.DMA((3,)),
                pltpu.SemaphoreType.DMA((groups, 2, CHUNKS)),
                pltpu.SemaphoreType.DMA((groups, 2, CHUNKS)),
                pltpu.SemaphoreType.DMA((n // 2, CHUNKS)),
                pltpu.SemaphoreType.DMA((n // 2, CHUNKS)),
                pltpu.SemaphoreType.DMA((n, CHUNKS)),
                pltpu.SemaphoreType.DMA((n, 2, CHUNKS)),
            ],
            compiler_params=pltpu.CompilerParams(collective_id=0, has_side_effects=True),
        )(local_weights, base_master, momentum)
        return new_master, new_momentum, all_rows.reshape(n * rows, width)

    return jax.shard_map(
        on_device,
        mesh=mesh,
        in_specs=(P("island", "fsdp", None), P("fsdp", None), P("fsdp", None)),
        out_specs=(P("fsdp", None), P("fsdp", None), P()),
        check_vma=False,
    )
```

```python
import functools

import jax
import jax.numpy as jnp
from jax import lax
from jax.experimental import pallas as pl
from jax.experimental.pallas import tpu as pltpu
from jax.sharding import PartitionSpec as P

BLOCK = 128
CHUNKS = 2
UNROLL = 8

epsilon = 1e-06
code_limit = 31.0
momentum_decay = 0.9
outer_rate = 0.7


def flip(index, mask):
    out = index
    bit = 1
    while bit <= mask:
        if mask & bit:
            out = out + bit - 2 * bit * lax.rem(lax.div(index, bit), 2)
        bit *= 2
    return out


def decoded(outer_grad):
    largest = jnp.max(jnp.abs(outer_grad), axis=1, keepdims=True)
    block_scale = (largest + epsilon) / code_limit
    coded = (outer_grad / block_scale).astype(jnp.bfloat16)
    return coded.astype(jnp.float32) * block_scale


def kernel(
    groups,
    n,
    weights_in,
    base_in,
    moment_in,
    master_out,
    moment_out,
    rows_out,
    weights,
    base,
    moment,
    load_sem,
    island_send,
    island_recv,
    line_send,
    pair_send,
    core_send,
    rows_recv,
):
    isl = lax.axis_index("island")
    shard = lax.axis_index("fsdp")
    mine = lax.rem(isl, 2)
    width = base.shape[1]
    half = width // 2
    piece = half // CHUNKS
    lines = range(2, n, 2)

    loads = [
        pltpu.make_async_copy(weights_in.at[0], weights.at[isl], load_sem.at[0]),
        pltpu.make_async_copy(base_in, base, load_sem.at[1]),
        pltpu.make_async_copy(moment_in, moment, load_sem.at[2]),
    ]
    for load in loads:
        load.start()

    barrier = pltpu.get_barrier_semaphore()
    partners = [(flip(isl, m), shard) for m in range(1, groups)]
    partners += [(isl, flip(shard, m)) for m in (1, *lines)]
    for partner in partners:
        pl.semaphore_signal(barrier, inc=1, device_id=partner, device_id_type=pl.DeviceIdType.MESH)
    loads[0].wait()
    pl.semaphore_wait(barrier, len(partners))

    def columns(side, k):
        return pl.ds(pl.multiple_of(side * half + k * piece, BLOCK), piece)

    def remote(ref, send, recv, partner):
        return pltpu.make_async_remote_copy(
            src_ref=ref,
            dst_ref=ref,
            send_sem=send,
            recv_sem=recv,
            device_id=partner,
            device_id_type=pl.DeviceIdType.MESH,
        )

    sent = []

    def send(copy):
        copy.start()
        sent.append(copy)

    def island_copy(source, side, k, mask, send_at, recv_at):
        return remote(
            weights.at[source, :, columns(side, k)],
            island_send.at[send_at],
            island_recv.at[recv_at],
            (flip(isl, mask), shard),
        )

    def rows_copy(mask, side, k, send_sem, recv_at, partner):
        return remote(
            rows_out.at[flip(shard, mask), :, columns(side, k)],
            send_sem,
            rows_recv.at[recv_at],
            partner,
        )

    for k in range(CHUNKS):
        for m in range(2, groups):
            side = mine if m % 2 == 0 else 1 - mine
            send(island_copy(isl, side, k, m, (m, 0, k), (m, 0, k)))
        send(island_copy(isl, 1 - mine, k, 1, (1, 0, k), (1, 0, k)))
    for k in range(CHUNKS):
        send(island_copy(isl, mine, k, 1, (1, 1, k), (1, 1, k)))
    loads[1].wait()
    loads[2].wait()

    def update(side, k):
        start = side * half + k * piece

        def step(t, carry):
            for u in range(UNROLL):
                at = pl.ds(pl.multiple_of(start + (t * UNROLL + u) * BLOCK, BLOCK), BLOCK)
                held = base[:, at]
                summed = None
                for m in range(groups):
                    term = decoded(held - weights[flip(isl, m), :, at].astype(jnp.float32))
                    summed = term if summed is None else summed + term
                averaged = summed / groups
                fresh_moment = momentum_decay * moment[:, at] + averaged
                fresh_master = held - outer_rate * (averaged + momentum_decay * fresh_moment)
                moment_out[:, at] = fresh_moment
                master_out[:, at] = fresh_master
                rows_out[shard, :, at] = fresh_master.astype(jnp.bfloat16)
            return carry

        lax.fori_loop(0, piece // (BLOCK * UNROLL), step, 0)

    def wait_island(mask, rel, k):
        island_copy(
            flip(isl, mask), mine if rel == 0 else 1 - mine, k, 1, (mask, rel, k), (mask, rel, k)
        ).wait_recv()

    def wait_rows(mask, rel, k):
        rows_copy(
            mask, mine if rel == 0 else 1 - mine, k, core_send.at[mask, k], (mask, rel, k), (flip(isl, 1), shard)
        ).wait_recv()

    pair = (isl, flip(shard, 1))
    core = (flip(isl, 1), shard)

    for k in range(CHUNKS):
        for m in range(1, groups):
            wait_island(m, 0, k)
            if m > 1:
                send(island_copy(flip(isl, m), mine, k, 1, (m, 1, k), (m ^ 1, 1, k)))
        update(mine, k)
        for m in lines:
            send(rows_copy(0, mine, k, line_send.at[m // 2, k], (m, 0, k), (isl, flip(shard, m))))
        send(rows_copy(0, mine, k, pair_send.at[0, k], (1, 0, k), pair))

    for k in range(CHUNKS):
        for m in range(1, groups):
            wait_island(m, 1, k)
        update(1 - mine, k)

    for k in range(CHUNKS):
        wait_rows(1, 0, k)
        send(rows_copy(1, mine, k, core_send.at[1, k], (1, 1, k), core))
        for m in lines:
            wait_rows(m, 0, k)
            send(rows_copy(m, mine, k, pair_send.at[m // 2, k], (m + 1, 0, k), pair))
            send(rows_copy(m, mine, k, core_send.at[m, k], (m, 1, k), core))
    for k in range(CHUNKS):
        for m in lines:
            wait_rows(m + 1, 0, k)
            send(rows_copy(m + 1, mine, k, core_send.at[m + 1, k], (m + 1, 1, k), core))
    for k in range(CHUNKS):
        for m in range(1, n):
            wait_rows(m, 1, k)
    for copy in sent:
        copy.wait_send()


def store(master, moment, rows, master_out, moment_out, rows_out, sems):
    copies = [
        pltpu.make_async_copy(rows, rows_out, sems.at[0]),
        pltpu.make_async_copy(master, master_out, sems.at[1]),
        pltpu.make_async_copy(moment, moment_out, sems.at[2]),
    ]
    for copy in copies:
        copy.start()
    for copy in copies:
        copy.wait()


def solution(mesh):
    groups, n = mesh.shape["island"], mesh.shape["fsdp"]

    def on_device(local_weights, base_master, momentum):
        rows, width = base_master.shape
        vmem = pl.BlockSpec(memory_space=pltpu.VMEM)
        hbm = pl.BlockSpec(memory_space=pltpu.HBM)
        new_master, new_momentum, all_rows = pl.pallas_call(
            functools.partial(kernel, groups, n),
            out_shape=(
                pltpu.VMEM((rows, width), jnp.float32),
                pltpu.VMEM((rows, width), jnp.float32),
                pltpu.VMEM((n, rows, width), jnp.bfloat16),
            ),
            in_specs=[hbm] * 3,
            out_specs=(vmem,) * 3,
            scratch_shapes=[
                pltpu.VMEM((groups, rows, width), jnp.bfloat16),
                pltpu.VMEM((rows, width), jnp.float32),
                pltpu.VMEM((rows, width), jnp.float32),
                pltpu.SemaphoreType.DMA((3,)),
                pltpu.SemaphoreType.DMA((groups, 2, CHUNKS)),
                pltpu.SemaphoreType.DMA((groups, 2, CHUNKS)),
                pltpu.SemaphoreType.DMA((n // 2, CHUNKS)),
                pltpu.SemaphoreType.DMA((n // 2, CHUNKS)),
                pltpu.SemaphoreType.DMA((n, CHUNKS)),
                pltpu.SemaphoreType.DMA((n, 2, CHUNKS)),
            ],
            compiler_params=pltpu.CompilerParams(
                collective_id=0, has_side_effects=True, vmem_limit_bytes=16 * 2**20
            ),
        )(local_weights, base_master, momentum)
        new_master, new_momentum, all_rows = pl.pallas_call(
            store,
            out_shape=tuple(
                pltpu.HBM(x.shape, x.dtype) for x in (new_master, new_momentum, all_rows)
            ),
            in_specs=[vmem] * 3,
            out_specs=(hbm,) * 3,
            scratch_shapes=[pltpu.SemaphoreType.DMA((3,))],
            compiler_params=pltpu.CompilerParams(vmem_limit_bytes=16 * 2**20),
        )(*(pltpu.with_memory_space_constraint(x, pltpu.VMEM) for x in (new_master, new_momentum, all_rows)))
        return new_master, new_momentum, all_rows.reshape(n * rows, width)

    return jax.shard_map(
        on_device,
        mesh=mesh,
        in_specs=(P("island", "fsdp", None), P("fsdp", None), P("fsdp", None)),
        out_specs=(P("fsdp", None), P("fsdp", None), P()),
        check_vma=False,
    )
```

```python
import functools

import jax
import jax.numpy as jnp
from jax import lax
from jax.experimental import pallas as pl
from jax.experimental.pallas import tpu as pltpu
from jax.sharding import PartitionSpec as P

BLOCK = 128
VMEM = 65472 * 2**10
GRANT = 60 * 1024 * 2**10
CHUNKS = 2
UNROLL = 8

epsilon = 1e-06
code_limit = 31.0
momentum_decay = 0.9
outer_rate = 0.7


def flip(index, mask):
    out = index
    bit = 1
    while bit <= mask:
        if mask & bit:
            out = out + bit - 2 * bit * lax.rem(lax.div(index, bit), 2)
        bit *= 2
    return out


def decoded(outer_grad):
    largest = jnp.max(jnp.abs(outer_grad), axis=1, keepdims=True)
    block_scale = (largest + epsilon) / code_limit
    coded = (outer_grad / block_scale).astype(jnp.bfloat16)
    return coded.astype(jnp.float32) * block_scale


def kernel(
    groups,
    n,
    weights_in,
    base_in,
    moment_in,
    master_out,
    moment_out,
    rows_out,
    weights,
    base,
    moment,
    load_sem,
    island_send,
    island_recv,
    line_send,
    pair_send,
    core_send,
    rows_recv,
):
    isl = lax.axis_index("island")
    shard = lax.axis_index("fsdp")
    mine = lax.rem(isl, 2)
    width = base.shape[1]
    half = width // 2
    piece = half // CHUNKS
    lines = range(2, n, 2)

    loads = [
        pltpu.make_async_copy(weights_in.at[0], weights.at[isl], load_sem.at[0]),
        pltpu.make_async_copy(base_in, base, load_sem.at[1]),
        pltpu.make_async_copy(moment_in, moment, load_sem.at[2]),
    ]
    for load in loads:
        load.start()

    barrier = pltpu.get_barrier_semaphore()
    partners = [(flip(isl, m), shard) for m in range(1, groups)]
    partners += [(isl, flip(shard, m)) for m in (1, *lines)]
    for partner in partners:
        pl.semaphore_signal(barrier, inc=1, device_id=partner, device_id_type=pl.DeviceIdType.MESH)
    loads[0].wait()
    pl.semaphore_wait(barrier, len(partners))

    def columns(side, k):
        return pl.ds(pl.multiple_of(side * half + k * piece, BLOCK), piece)

    def remote(ref, send, recv, partner):
        return pltpu.make_async_remote_copy(
            src_ref=ref,
            dst_ref=ref,
            send_sem=send,
            recv_sem=recv,
            device_id=partner,
            device_id_type=pl.DeviceIdType.MESH,
        )

    sent = []

    def send(copy):
        copy.start()
        sent.append(copy)

    def island_copy(source, side, k, mask, send_at, recv_at):
        return remote(
            weights.at[source, :, columns(side, k)],
            island_send.at[send_at],
            island_recv.at[recv_at],
            (flip(isl, mask), shard),
        )

    def rows_copy(mask, side, k, send_sem, recv_at, partner):
        return remote(
            rows_out.at[flip(shard, mask), :, columns(side, k)],
            send_sem,
            rows_recv.at[recv_at],
            partner,
        )

    for k in range(CHUNKS):
        for m in range(2, groups):
            side = mine if m % 2 == 0 else 1 - mine
            send(island_copy(isl, side, k, m, (m, 0, k), (m, 0, k)))
        send(island_copy(isl, 1 - mine, k, 1, (1, 0, k), (1, 0, k)))
    for k in range(CHUNKS):
        send(island_copy(isl, mine, k, 1, (1, 1, k), (1, 1, k)))
    loads[1].wait()
    loads[2].wait()

    def update(side, k):
        start = side * half + k * piece

        def step(t, carry):
            for u in range(UNROLL):
                at = pl.ds(pl.multiple_of(start + (t * UNROLL + u) * BLOCK, BLOCK), BLOCK)
                held = base[:, at]
                summed = None
                for m in range(groups):
                    term = decoded(held - weights[flip(isl, m), :, at].astype(jnp.float32))
                    summed = term if summed is None else summed + term
                averaged = summed / groups
                fresh_moment = momentum_decay * moment[:, at] + averaged
                fresh_master = held - outer_rate * (averaged + momentum_decay * fresh_moment)
                moment_out[:, at] = fresh_moment
                master_out[:, at] = fresh_master
                rows_out[shard, :, at] = fresh_master.astype(jnp.bfloat16)
            return carry

        lax.fori_loop(0, piece // (BLOCK * UNROLL), step, 0)

    def wait_island(mask, rel, k):
        island_copy(
            flip(isl, mask), mine if rel == 0 else 1 - mine, k, 1, (mask, rel, k), (mask, rel, k)
        ).wait_recv()

    def wait_rows(mask, rel, k):
        rows_copy(
            mask, mine if rel == 0 else 1 - mine, k, core_send.at[mask, k], (mask, rel, k), (flip(isl, 1), shard)
        ).wait_recv()

    pair = (isl, flip(shard, 1))
    core = (flip(isl, 1), shard)

    for k in range(CHUNKS):
        for m in range(1, groups):
            wait_island(m, 0, k)
            if m > 1:
                send(island_copy(flip(isl, m), mine, k, 1, (m, 1, k), (m ^ 1, 1, k)))
        update(mine, k)
        for m in lines:
            send(rows_copy(0, mine, k, line_send.at[m // 2, k], (m, 0, k), (isl, flip(shard, m))))
        send(rows_copy(0, mine, k, pair_send.at[0, k], (1, 0, k), pair))

    for k in range(CHUNKS):
        for m in range(1, groups):
            wait_island(m, 1, k)
        update(1 - mine, k)

    for k in range(CHUNKS):
        wait_rows(1, 0, k)
        send(rows_copy(1, mine, k, core_send.at[1, k], (1, 1, k), core))
        for m in lines:
            wait_rows(m, 0, k)
            send(rows_copy(m, mine, k, pair_send.at[m // 2, k], (m + 1, 0, k), pair))
            send(rows_copy(m, mine, k, core_send.at[m, k], (m, 1, k), core))
    for k in range(CHUNKS):
        for m in lines:
            wait_rows(m + 1, 0, k)
            send(rows_copy(m + 1, mine, k, core_send.at[m + 1, k], (m + 1, 1, k), core))
    for k in range(CHUNKS):
        for m in range(1, n):
            wait_rows(m, 1, k)
    for copy in sent:
        copy.wait_send()


def store(master, moment, rows, master_out, moment_out, rows_out, sems):
    copies = [
        pltpu.make_async_copy(rows, rows_out, sems.at[0]),
        pltpu.make_async_copy(master, master_out, sems.at[1]),
        pltpu.make_async_copy(moment, moment_out, sems.at[2]),
    ]
    for copy in copies:
        copy.start()
    for copy in copies:
        copy.wait()


def solution(mesh):
    groups, n = mesh.shape["island"], mesh.shape["fsdp"]

    def on_device(local_weights, base_master, momentum):
        rows, width = base_master.shape
        held = rows * width * (2 * 4 + n * 2)
        grant = min(GRANT, VMEM - held - 2**20)
        vmem = pl.BlockSpec(memory_space=pltpu.VMEM)
        hbm = pl.BlockSpec(memory_space=pltpu.HBM)
        new_master, new_momentum, all_rows = pl.pallas_call(
            functools.partial(kernel, groups, n),
            out_shape=(
                pltpu.VMEM((rows, width), jnp.float32),
                pltpu.VMEM((rows, width), jnp.float32),
                pltpu.VMEM((n, rows, width), jnp.bfloat16),
            ),
            in_specs=[hbm] * 3,
            out_specs=(vmem,) * 3,
            scratch_shapes=[
                pltpu.VMEM((groups, rows, width), jnp.bfloat16),
                pltpu.VMEM((rows, width), jnp.float32),
                pltpu.VMEM((rows, width), jnp.float32),
                pltpu.SemaphoreType.DMA((3,)),
                pltpu.SemaphoreType.DMA((groups, 2, CHUNKS)),
                pltpu.SemaphoreType.DMA((groups, 2, CHUNKS)),
                pltpu.SemaphoreType.DMA((n // 2, CHUNKS)),
                pltpu.SemaphoreType.DMA((n // 2, CHUNKS)),
                pltpu.SemaphoreType.DMA((n, CHUNKS)),
                pltpu.SemaphoreType.DMA((n, 2, CHUNKS)),
            ],
            compiler_params=pltpu.CompilerParams(
                collective_id=0, has_side_effects=True, vmem_limit_bytes=grant
            ),
        )(local_weights, base_master, momentum)
        new_master, new_momentum, all_rows = pl.pallas_call(
            store,
            out_shape=tuple(
                pltpu.HBM(x.shape, x.dtype) for x in (new_master, new_momentum, all_rows)
            ),
            in_specs=[vmem] * 3,
            out_specs=(hbm,) * 3,
            scratch_shapes=[pltpu.SemaphoreType.DMA((3,))],
            compiler_params=pltpu.CompilerParams(vmem_limit_bytes=grant),
        )(*(pltpu.with_memory_space_constraint(x, pltpu.VMEM) for x in (new_master, new_momentum, all_rows)))
        return new_master, new_momentum, all_rows.reshape(n * rows, width)

    return jax.shard_map(
        on_device,
        mesh=mesh,
        in_specs=(P("island", "fsdp", None), P("fsdp", None), P("fsdp", None)),
        out_specs=(P("fsdp", None), P("fsdp", None), P()),
        check_vma=False,
    )
```
